256 devices in a mesh: dp: 4 (over x_hi, core), row: 8 (over z), col: 8 (over x_lo, y).
Axes of the slice: x: 4 (x_hi: 2, x_lo: 2; x = x_hi * 2 + x_lo), y: 4, z: 8, core: 2. Of those that a mesh axis runs over, the one named last changes fastest.
Arguments:
- tokens: bfloat16 [4096, 4096], P(('dp', 'col'), 'row'), may hold values from -6 to 6
- cotangent: bfloat16 [4096, 4096], P(('dp', 'col'), 'row'), may hold values from -6 to 6
- gate_pre: bfloat16 [4096, 14336], P(('dp', 'row'), 'col'), may hold values from -6 to 6
- up_pre: bfloat16 [4096, 14336], P(('dp', 'row'), 'col'), may hold values from -6 to 6
- w_gate: bfloat16 [14336, 4096], P('col', 'row'), may hold values from -0.09375 to 0.09375
- w_up: bfloat16 [14336, 4096], P('col', 'row'), may hold values from -0.09375 to 0.09375
- w_down: bfloat16 [4096, 14336], P('row', 'col'), may hold values from -0.046875 to 0.046875
Outputs:
- d_tokens: bfloat16 [4096, 4096], P(('dp', 'col'), 'row')
- grad_gate: float32 [14336, 4096], P(('col', 'dp'), 'row')
- grad_up: float32 [14336, 4096], P(('col', 'dp'), 'row')
- grad_down: float32 [4096, 14336], P(('row', 'dp'), 'col')
The draws below stay inside these ranges and needn't reach their ends.
All inputs are finite; a program needn't handle non-finite values.
Results may differ from the reference program's by a relative error of at most 0.02.
Values may be sent and summed in bfloat16 or wider, within the bound.
No kernel may reach another device: no remote copies, remote signals or barrier semaphores. Data moves between devices by JAX's collectives and lax.ppermute only.
A program may use at most 128 MiB of HBM per device.

```python
import jax
import jax.numpy as jnp
from jax import lax

D = 4096
FF = 14336
TOKENS = 4096
N_ROW = 8


def strengthened(array, rng, source, target, shards_of, factor):
    def block_of(axis_at):
        return (jnp.arange(array.shape[axis_at]) // (array.shape[axis_at] // shards_of)).reshape((-1,) + (1,) * (array.ndim - 1 - axis_at))

    near = jax.random.permutation(rng, shards_of)[block_of(target)]
    far = (block_of(target) + shards_of // 2) % shards_of
    return jnp.where((block_of(source) == near) | (block_of(source) == far), factor * array, array)


def levels(key, shape, pieces, low, largest):
    gain = 1.0
    for position, blocks in pieces:
        steps = jax.random.uniform(jax.random.fold_in(jax.random.fold_in(key, 6), position), (blocks,), jnp.float32, low / len(pieces), largest / len(pieces))
        gain = gain * jnp.repeat(jnp.exp(steps), shape[position] // blocks).reshape((-1,) + (1,) * (len(shape) - 1 - position))
    return gain


def noise(rng, shape, spread, limit, shards=(), dtype=jnp.bfloat16):
    values = spread * jax.random.normal(rng, shape, jnp.float32)
    if shards:
        values = values * levels(rng, shape, shards, -0.22, 0.18)
    return jnp.clip(values, -limit, limit).astype(dtype)


def bell_draw_with(own_key, extent, width, most, shards, heavy, kind=jnp.bfloat16):
    drawn = width * jax.random.normal(own_key, extent, jnp.float32)
    if shards:
        drawn = drawn * levels(own_key, extent, shards, -0.22, 0.18)
    return jnp.clip(strengthened(drawn, jax.random.fold_in(own_key, 3), *heavy), -most, most).astype(kind)


def setup_inputs(seed: int = 0) -> dict:
    seeds = jax.random.split(jax.random.key(seed), 8)
    return {
        "tokens": noise(seeds[0], (TOKENS, D), 1.0, 6.0, ((0, 32), (1, 8))),
        "cotangent": bell_draw_with(seeds[1], (TOKENS, D), 1.0, 6.0, ((0, 32), (1, 8)), (0, 1, 32, 2.75)),
        "gate_pre": noise(seeds[2], (TOKENS, FF), 1.5, 6.0, ((0, 32), (1, 8))),
        "up_pre": noise(seeds[3], (TOKENS, FF), 1.0, 6.0, ((0, 32), (1, 8))),
        "w_gate": noise(seeds[4], (FF, D), D ** -0.5, 0.09375, ((0, 8), (1, 8))),
        "w_up": noise(seeds[5], (FF, D), D ** -0.5, 0.09375, ((0, 8), (1, 8))),
        "w_down": noise(seeds[6], (D, FF), FF ** -0.5, 0.046875, ((0, 8), (1, 8))),
    }


def reference(tokens, cotangent, gate_pre, up_pre, w_gate, w_up, w_down):
    block_width = D // N_ROW
    cot_blocks = jnp.transpose(cotangent.reshape(TOKENS, N_ROW, block_width), (1, 0, 2))
    down_blocks = w_down.reshape(N_ROW, block_width, FF)

    def accumulate(running, block_pair):
        cot_block, down_block = block_pair
        product = jnp.dot(cot_block, down_block, preferred_element_type=jnp.float32)
        rounded = lax.optimization_barrier(product.astype(jnp.bfloat16))
        return running + rounded.astype(jnp.float32), None

    hidden_grad, _ = lax.scan(accumulate, jnp.zeros((TOKENS, FF), jnp.float32), (cot_blocks, down_blocks))
    gate_value = gate_pre.astype(jnp.float32)
    up_value = up_pre.astype(jnp.float32)
    sigmoid_gate = jax.nn.sigmoid(gate_value)
    hidden = (gate_value * sigmoid_gate * up_value).astype(jnp.bfloat16)
    gate_grad = (hidden_grad * up_value * sigmoid_gate * (1.0 + gate_value * (1.0 - sigmoid_gate))).astype(jnp.bfloat16)
    up_grad = (hidden_grad * gate_value * sigmoid_gate).astype(jnp.bfloat16)
    d_tokens = (jnp.dot(gate_grad, w_gate, preferred_element_type=jnp.float32) + jnp.dot(up_grad, w_up, preferred_element_type=jnp.float32)).astype(jnp.bfloat16)
    grad_gate = jnp.dot(gate_grad.T, tokens, preferred_element_type=jnp.float32)
    grad_up = jnp.dot(up_grad.T, tokens, preferred_element_type=jnp.float32)
    grad_down = jnp.dot(cotangent.T, hidden, preferred_element_type=jnp.float32)
    return (d_tokens, grad_gate, grad_up, grad_down)
```

```python
import jax
import jax.numpy as jnp
from jax import lax
from jax.sharding import PartitionSpec as P

F32 = jnp.float32
BF16 = jnp.bfloat16
ROWS = 8
CHUNKS = 2


def shift_row(x, step):
    return lax.ppermute(x, "row", [(i, (i + step) % ROWS) for i in range(ROWS)])


def shift_y(x, step):
    return lax.ppermute(
        x, "col", [(a * 4 + b, a * 4 + (b + step) % 4) for a in range(2) for b in range(4)]
    )


def swap_x(x):
    return lax.ppermute(x, "col", [(i, (i + 4) % 8) for i in range(8)])


def swap_core(x):
    return lax.ppermute(x, "dp", [(0, 1), (1, 0), (2, 3), (3, 2)])


def swap_far(x):
    return lax.ppermute(x, "dp", [(0, 2), (2, 0), (1, 3), (3, 1)])


def gather_row(x):
    half = x.shape[0] // 2
    blocks = [None] * ROWS
    blocks[0] = up = down = x
    for step in range(1, 4):
        up, down = shift_row(up, 1), shift_row(down, -1)
        blocks[ROWS - step], blocks[step] = up, down
    blocks[4] = jnp.concatenate([shift_row(up[:half], 1), shift_row(down[half:], -1)], axis=0)
    return blocks


def reduce_row(parts):
    half = parts[0].shape[0] // 2

    def add(a, b):
        return (a.astype(F32) + b.astype(F32)).astype(BF16)

    up = shift_row(parts[4][:half], 1)
    down = shift_row(parts[4][half:], -1)
    up = shift_row(jnp.concatenate([add(parts[3][:half], up), parts[3][half:]], axis=0), 1)
    down = shift_row(jnp.concatenate([parts[5][:half], add(parts[5][half:], down)], axis=0), -1)
    up = shift_row(add(parts[2], up), 1)
    down = shift_row(add(parts[6], down), -1)
    up = shift_row(add(parts[1], up), 1)
    down = shift_row(add(parts[7], down), -1)
    return parts[0].astype(F32) + up.astype(F32) + down.astype(F32)


def gather_col(x, row, x_at, y_at):
    pair = jnp.stack([x, swap_x(x)])
    down, up = shift_y(pair, -1), shift_y(pair, 1)
    far = jnp.stack([shift_y(up[0], 1), shift_y(down[1], -1)])
    blocks = jnp.concatenate([pair, down, far, up], axis=0)
    picked = []
    for o in range(ROWS):
        block = (row + o) % ROWS
        at = ((block % 4 - y_at) % 4) * 2 + (block // 4 + x_at) % 2
        picked.append(lax.dynamic_index_in_dim(blocks, at, 0, keepdims=False))
    return jnp.concatenate(picked, axis=0)


def contract_tokens(left, right):
    return lax.dot_general(left, right, (((0,), (0,)), ((), ())), preferred_element_type=F32)


def local(tokens, cotangent, gate_pre, up_pre, w_gate, w_up, w_down):
    row = lax.axis_index("row")
    col = lax.axis_index("col")
    dp = lax.axis_index("dp")
    x_at, y_at = col // 4, col % 4
    far_at, core_at = dp // 2, dp % 2
    hidden_width = gate_pre.shape[1]
    width = hidden_width // CHUNKS
    block = gate_pre.shape[0]

    gate_value = gate_pre.astype(F32)
    up_value = up_pre.astype(F32)
    sigmoid_gate = jax.nn.sigmoid(gate_value)
    hidden = (gate_value * sigmoid_gate * up_value).astype(BF16)
    gate_factor = up_value * sigmoid_gate * (1.0 + gate_value * (1.0 - sigmoid_gate))
    up_factor = gate_value * sigmoid_gate

    cot = gather_col(cotangent, row, x_at, y_at)
    hidden_all = [
        jnp.concatenate(gather_row(hidden[:, k * width : (k + 1) * width]), axis=0)
        for k in range(CHUNKS)
    ]
    tok = gather_col(tokens, row, x_at, y_at)

    token_grad = 0.0
    grads = []
    downs = []
    for k in range(CHUNKS):
        cols = slice(k * width, (k + 1) * width)
        partial = jnp.dot(cot, w_down[:, cols], preferred_element_type=F32).astype(BF16)
        parts = [partial[o * block : (o + 1) * block] for o in range(ROWS)]
        hidden_grad = reduce_row(parts)
        gate_grad = (hidden_grad * gate_factor[:, cols]).astype(BF16)
        up_grad = (hidden_grad * up_factor[:, cols]).astype(BF16)
        gate_all = jnp.concatenate(gather_row(gate_grad), axis=0)
        up_all = jnp.concatenate(gather_row(up_grad), axis=0)
        token_grad = (
            token_grad
            + jnp.dot(gate_all, w_gate[cols], preferred_element_type=F32)
            + jnp.dot(up_all, w_up[cols], preferred_element_type=F32)
        )
        stacked = jnp.stack([contract_tokens(gate_all, tok), contract_tokens(up_all, tok)])
        owned = stacked.reshape(2, 2, width // 2, stacked.shape[-1])
        other = lax.dynamic_index_in_dim(owned, 1 - core_at, 1, keepdims=False).astype(BF16)
        mine = lax.dynamic_index_in_dim(owned, core_at, 1, keepdims=False)
        mine = mine + swap_core(other).astype(F32)
        perm = [(2, 0), (3, 1)] if k == 0 else [(0, 2), (1, 3)]
        grads.append(mine + lax.ppermute(mine.astype(BF16), "dp", perm).astype(F32))

        down = contract_tokens(cot, hidden_all[k]).reshape(2, 2, block, width)
        other = lax.dynamic_index_in_dim(down, 1 - core_at, 1, keepdims=False).astype(BF16)
        mine = lax.dynamic_index_in_dim(down, core_at, 1, keepdims=False)
        mine = mine + swap_core(other).astype(F32)
        away = lax.dynamic_index_in_dim(mine, 1 - far_at, 0, keepdims=False).astype(BF16)
        mine = lax.dynamic_index_in_dim(mine, far_at, 0, keepdims=False)
        downs.append(mine + swap_far(away).astype(F32))

    owned = jnp.where(far_at == 0, grads[0], grads[1])
    grad_down = jnp.concatenate(downs, axis=1)

    token_grad = token_grad.reshape(ROWS, block, token_grad.shape[-1])

    def at_y(step):
        y = (y_at + step) % 4
        return jnp.stack(
            [
                lax.dynamic_index_in_dim(token_grad, (a * 4 + y - row) % ROWS, 0, keepdims=False)
                for a in range(2)
            ]
        )

    mine = (
        at_y(0)
        + shift_y(at_y(1).astype(BF16), 1).astype(F32)
        + shift_y(at_y(3).astype(BF16), -1).astype(F32)
        + shift_y(at_y(2).astype(BF16), 2).astype(F32)
    )
    away = lax.dynamic_index_in_dim(mine, 1 - x_at, 0, keepdims=False).astype(BF16)
    mine = lax.dynamic_index_in_dim(mine, x_at, 0, keepdims=False)
    d_tokens = (mine + swap_x(away).astype(F32)).astype(BF16)
    return (d_tokens, owned[0], owned[1], grad_down)


def solution(mesh):
    placed = (
        P(("dp", "col"), "row"),
        P(("dp", "col"), "row"),
        P(("dp", "row"), "col"),
        P(("dp", "row"), "col"),
        P("col", "row"),
        P("col", "row"),
        P("row", "col"),
    )
    return jax.shard_map(
        local,
        mesh=mesh,
        in_specs=placed,
        out_specs=(
            P(("dp", "col"), "row"),
            P(("col", "dp"), "row"),
            P(("col", "dp"), "row"),
            P(("row", "dp"), "col"),
        ),
        check_vma=False,
    )
```

```python
import jax
import jax.numpy as jnp
from jax import lax
from jax.sharding import PartitionSpec as P

F32 = jnp.float32
BF16 = jnp.bfloat16
ROWS = 8


def shift_row(x, step):
    return lax.ppermute(x, "row", [(i, (i + step) % ROWS) for i in range(ROWS)])


def shift_y(x, step):
    return lax.ppermute(
        x, "col", [(a * 4 + b, a * 4 + (b + step) % 4) for a in range(2) for b in range(4)]
    )


def swap_x(x):
    return lax.ppermute(x, "col", [(i, (i + 4) % 8) for i in range(8)])


def swap_core(x):
    return lax.ppermute(x, "dp", [(0, 1), (1, 0), (2, 3), (3, 2)])


def swap_far(x):
    return lax.ppermute(x, "dp", [(0, 2), (2, 0), (1, 3), (3, 1)])


def gather_row(x, sign, gates=None):
    blocks = [None] * ROWS
    blocks[0] = up = down = x
    for step in range(1, 5):
        if gates is not None and gates[step - 1] is not None:
            up, down, _ = lax.optimization_barrier((up, down, gates[step - 1]))
        if step < 4 or sign > 0:
            up = shift_row(up, 1)
            blocks[ROWS - step] = up
        if step < 4 or sign < 0:
            down = shift_row(down, -1)
            blocks[step] = down
    return blocks


def reduce_row(part, sign):
    def add(o, b):
        return (part(o).astype(F32) + b.astype(F32)).astype(BF16)

    up = shift_row(part(4), 1) if sign > 0 else None
    down = shift_row(part(4), -1) if sign < 0 else None
    for step in (3, 2, 1):
        up = shift_row(part(step) if up is None else add(step, up), 1)
        down = shift_row(part(ROWS - step) if down is None else add(ROWS - step, down), -1)
    return part(0).astype(F32) + up.astype(F32) + down.astype(F32)


def gather_col(x, x_at, y_at):
    pair = jnp.stack([x, swap_x(x)])
    blocks = jnp.concatenate([pair, shift_y(pair, -1), shift_y(pair, 2), shift_y(pair, 1)], axis=0)
    picked = []
    for block in range(8):
        at = ((block % 4 - y_at) % 4) * 2 + (block // 4 + x_at) % 2
        picked.append(lax.dynamic_index_in_dim(blocks, at, 0, keepdims=False))
    return jnp.concatenate(picked, axis=0)


def contract_tokens(left, right):
    return lax.dot_general(left, right, (((0,), (0,)), ((), ())), preferred_element_type=F32)


def pick(x, at, axis):
    return lax.dynamic_index_in_dim(x, at, axis, keepdims=False)


def local(tokens, cotangent, gate_pre, up_pre, w_gate, w_up, w_down):
    row = lax.axis_index("row")
    col = lax.axis_index("col")
    dp = lax.axis_index("dp")
    x_at, y_at = col // 4, col % 4
    far_at, core_at = dp // 2, dp % 2
    block, hidden_width = gate_pre.shape
    features = w_gate.shape[1]
    owned = hidden_width // 4
    ends = ((128, owned), (0, 128))

    def columns(x, k, axis):
        low, high = ends[k]
        return jnp.concatenate(
            [lax.slice_in_dim(x, d * owned + low, d * owned + high, axis=axis) for d in range(4)],
            axis=axis,
        )

    gate_value = gate_pre.astype(F32)
    up_value = up_pre.astype(F32)
    hidden = (gate_value * jax.nn.sigmoid(gate_value) * up_value).astype(BF16)
    hidden_all = lax.all_gather(hidden, "row", axis=0, tiled=True)
    cot = gather_col(cotangent, x_at, y_at)
    tok = lax.all_gather(tokens, "col", axis=0, tiled=True)
    tok = jnp.concatenate([tok, tok], axis=0)
    tok = lax.dynamic_slice_in_dim(tok, row * block, ROWS * block, 0)

    token_grad = []
    grads = []
    gates = None
    for k, sign in ((0, 1), (1, -1)):
        partial = jnp.dot(cot, columns(w_down, k, 1), preferred_element_type=F32).astype(BF16)
        partial = partial.reshape(ROWS, block, partial.shape[-1])
        hidden_grad = reduce_row(lambda o: pick(partial, (row + o) % ROWS, 0), sign)
        gate_value = columns(gate_pre, k, 1).astype(F32)
        up_value = columns(up_pre, k, 1).astype(F32)
        sigmoid_gate = jax.nn.sigmoid(gate_value)
        gate_grad = (
            hidden_grad * up_value * sigmoid_gate * (1.0 + gate_value * (1.0 - sigmoid_gate))
        ).astype(BF16)
        up_grad = (hidden_grad * gate_value * sigmoid_gate).astype(BF16)
        blocks = gather_row(jnp.stack([gate_grad, up_grad]), sign, gates)
        gates = [blocks[6], blocks[5], blocks[4], None]
        gate_all = jnp.concatenate([b[0] for b in blocks], axis=0)
        up_all = jnp.concatenate([b[1] for b in blocks], axis=0)
        stacked = jnp.stack([contract_tokens(gate_all, tok), contract_tokens(up_all, tok)])
        stacked = stacked.reshape(2, 2, 2, -1, features)
        other = pick(stacked, 1 - core_at, 2).astype(BF16)
        mine = pick(stacked, core_at, 2) + swap_core(other).astype(F32)
        away = pick(mine, 1 - far_at, 1).astype(BF16)
        grads.append(pick(mine, far_at, 1) + swap_far(away).astype(F32))
        token_grad.append(
            jnp.dot(gate_all, columns(w_gate, k, 0), preferred_element_type=F32)
            + jnp.dot(up_all, columns(w_up, k, 0), preferred_element_type=F32)
        )

    down = contract_tokens(cot, hidden_all).reshape(2, 2, block, hidden_width)
    other = pick(down, 1 - core_at, 1).astype(BF16)
    mine = pick(down, core_at, 1) + swap_core(other).astype(F32)
    away = pick(mine, 1 - far_at, 0).astype(BF16)
    grad_down = pick(mine, far_at, 0) + swap_far(away).astype(F32)

    token_grad = (token_grad[0] + token_grad[1]).reshape(ROWS, block, features)

    def at_y(step):
        y = (y_at + step) % 4
        return jnp.stack([pick(token_grad, (a * 4 + y - row) % ROWS, 0) for a in range(2)])

    mine = (
        at_y(0)
        + shift_y(at_y(1).astype(BF16), 1).astype(F32)
        + shift_y(at_y(3).astype(BF16), -1).astype(F32)
        + shift_y(at_y(2).astype(BF16), 2).astype(F32)
    )
    away = pick(mine, 1 - x_at, 0).astype(BF16)
    d_tokens = (pick(mine, x_at, 0) + swap_x(away).astype(F32)).astype(BF16)
    grad_gate = jnp.concatenate([grads[1][0], grads[0][0]], axis=0)
    grad_up = jnp.concatenate([grads[1][1], grads[0][1]], axis=0)
    return (d_tokens, grad_gate, grad_up, grad_down)


def solution(mesh):
    placed = (
        P(("dp", "col"), "row"),
        P(("dp", "col"), "row"),
        P(("dp", "row"), "col"),
        P(("dp", "row"), "col"),
        P("col", "row"),
        P("col", "row"),
        P("row", "col"),
    )
    return jax.shard_map(
        local,
        mesh=mesh,
        in_specs=placed,
        out_specs=(
            P(("dp", "col"), "row"),
            P(("col", "dp"), "row"),
            P(("col", "dp"), "row"),
            P(("row", "dp"), "col"),
        ),
        check_vma=False,
    )
```

```python
import jax
import jax.numpy as jnp
from jax import lax
from jax.sharding import PartitionSpec as P

F32 = jnp.float32
BF16 = jnp.bfloat16
ROWS = 8


def shift_row(x, step):
    return lax.ppermute(x, "row", [(i, (i + step) % ROWS) for i in range(ROWS)])


def exchange(x, axis, groups=None):
    return lax.all_to_all(x, axis, 0, 0, axis_index_groups=groups, tiled=True)


def gather_col(x):
    return exchange(jnp.broadcast_to(x, (8,) + x.shape), "col").reshape(-1, x.shape[-1])


def sum_dp(x):
    near = exchange(jnp.swapaxes(x.astype(BF16), 0, 1), "dp", [[0, 1], [2, 3]])
    half = (near[0].astype(F32) + near[1].astype(F32)).astype(BF16)
    far = exchange(half, "dp", [[0, 2], [1, 3]])
    return far[0].astype(F32) + far[1].astype(F32)


def gather_row(x, sign):
    blocks = [None] * ROWS
    blocks[0] = up = down = x
    for step in range(1, 5):
        if step < 4 or sign > 0:
            up = shift_row(up, 1)
            blocks[ROWS - step] = up
        if step < 4 or sign < 0:
            down = shift_row(down, -1)
            blocks[step] = down
    return blocks


def contract_tokens(left, right):
    return lax.dot_general(left, right, (((0,), (0,)), ((), ())), preferred_element_type=F32)


def local(tokens, cotangent, gate_pre, up_pre, w_gate, w_up, w_down):
    row = lax.axis_index("row")
    block, hidden_width = gate_pre.shape
    features = w_gate.shape[1]

    def turned(x, by):
        twice = jnp.concatenate([x, x], axis=0)
        return lax.dynamic_slice_in_dim(twice, by * block, ROWS * block, 0)

    gate_value = gate_pre.astype(F32)
    up_value = up_pre.astype(F32)
    sigmoid_gate = jax.nn.sigmoid(gate_value)
    hidden = (gate_value * sigmoid_gate * up_value).astype(BF16)
    hidden_blocks = gather_row(hidden, 1)

    cot = gather_col(cotangent)
    cot, hidden_blocks[1], hidden_blocks[7] = lax.optimization_barrier(
        (cot, hidden_blocks[1], hidden_blocks[7])
    )
    partial = jnp.dot(cot, w_down, preferred_element_type=F32).astype(BF16)
    partial, tokens = lax.optimization_barrier((partial, tokens))
    hidden_grad = lax.psum_scatter(partial, "row", scatter_dimension=0, tiled=True)
    hidden_grad, *hidden_blocks = lax.optimization_barrier((hidden_grad, *hidden_blocks))
    hidden_grad = hidden_grad.astype(F32)
    gate_grad = (
        hidden_grad * up_value * sigmoid_gate * (1.0 + gate_value * (1.0 - sigmoid_gate))
    ).astype(BF16)
    up_grad = (hidden_grad * gate_value * sigmoid_gate).astype(BF16)
    gate_all = lax.all_gather(gate_grad, "row", axis=0, tiled=True)
    up_all = jnp.concatenate(gather_row(up_grad, -1), axis=0)

    hidden_all = jnp.concatenate(hidden_blocks, axis=0)
    grad_down = sum_dp(
        contract_tokens(turned(cot, row), hidden_all).reshape(2, 2, block, hidden_width)
    )
    tok = gather_col(tokens)
    grad_up = sum_dp(contract_tokens(up_all, turned(tok, row)).reshape(2, 2, -1, features))
    grad_gate = sum_dp(contract_tokens(gate_all, tok).reshape(2, 2, -1, features))
    from_up = jnp.dot(up_all, w_up, preferred_element_type=F32)
    from_gate = jnp.dot(gate_all, w_gate, preferred_element_type=F32)
    token_grad = (from_gate + turned(from_up, (ROWS - row) & 7)).astype(BF16)
    token_grad = exchange(token_grad.reshape(8, block, features), "col")
    d_tokens = jnp.sum(token_grad.astype(F32), axis=0).astype(BF16)
    return (d_tokens, grad_gate, grad_up, grad_down)


def solution(mesh):
    placed = (
        P(("dp", "col"), "row"),
        P(("dp", "col"), "row"),
        P(("dp", "row"), "col"),
        P(("dp", "row"), "col"),
        P("col", "row"),
        P("col", "row"),
        P("row", "col"),
    )
    return jax.shard_map(
        local,
        mesh=mesh,
        in_specs=placed,
        out_specs=(
            P(("dp", "col"), "row"),
            P(("col", "dp"), "row"),
            P(("col", "dp"), "row"),
            P(("row", "dp"), "col"),
        ),
        check_vma=False,
    )
```

```python
import jax
import jax.numpy as jnp
from jax import lax
from jax.sharding import PartitionSpec as P

F32 = jnp.float32
BF16 = jnp.bfloat16
ROWS = 8


def shift_row(x, step):
    return lax.ppermute(x, "row", [(i, (i + step) % ROWS) for i in range(ROWS)])


def exchange(x, axis, groups=None):
    return lax.all_to_all(x, axis, 0, 0, axis_index_groups=groups, tiled=True)


def gather_col(x):
    return exchange(jnp.broadcast_to(x, (8,) + x.shape), "col").reshape(-1, x.shape[-1])


def pick(x, at, axis):
    return lax.dynamic_index_in_dim(x, at, axis, keepdims=False)


def halve_core(x, core):
    other = lax.ppermute(
        pick(x, 1 - core, 1).astype(BF16), "dp", [(0, 1), (1, 0), (2, 3), (3, 2)]
    )
    return pick(x, core, 1) + other.astype(F32)


def swap_far(x):
    return lax.ppermute(x, "dp", [(0, 2), (2, 0), (1, 3), (3, 1)])


def swap_x(x):
    return lax.ppermute(x, "col", [(i, (i + 4) % 8) for i in range(8)])


def gather_row(x, sign):
    blocks = [None] * ROWS
    blocks[0] = up = down = x
    for step in range(1, 5):
        if step < 4 or sign > 0:
            up = shift_row(up, 1)
            blocks[ROWS - step] = up
        if step < 4 or sign < 0:
            down = shift_row(down, -1)
            blocks[step] = down
    return blocks


def contract_tokens(left, right):
    return lax.dot_general(left, right, (((0,), (0,)), ((), ())), preferred_element_type=F32)


def local(tokens, cotangent, gate_pre, up_pre, w_gate, w_up, w_down):
    row = lax.axis_index("row")
    dp = lax.axis_index("dp")
    far, core = dp >> 1, dp & 1
    x_at = lax.axis_index("col") >> 2
    block, hidden_width = gate_pre.shape
    features = w_gate.shape[1]

    def turned(x, by):
        twice = jnp.concatenate([x, x], axis=0)
        return lax.dynamic_slice_in_dim(twice, by * block, ROWS * block, 0)

    gate_value = gate_pre.astype(F32)
    up_value = up_pre.astype(F32)
    sigmoid_gate = jax.nn.sigmoid(gate_value)
    hidden = (gate_value * sigmoid_gate * up_value).astype(BF16)
    hidden_blocks = gather_row(hidden, 1)

    cot = gather_col(cotangent)
    early = [hidden_blocks[o] for o in (1, 2, 6, 7)]
    cot, *early = lax.optimization_barrier((cot, *early))
    hidden_blocks[1:3], hidden_blocks[6:] = early[:2], early[2:]
    partial = jnp.dot(cot, w_down, preferred_element_type=F32).astype(BF16)
    partial, tokens = lax.optimization_barrier((partial, tokens))
    tok = gather_col(tokens)
    hidden_grad = lax.psum_scatter(partial, "row", scatter_dimension=0, tiled=True)
    hidden_grad, tok, *hidden_blocks = lax.optimization_barrier((hidden_grad, tok, *hidden_blocks))
    hidden_grad = hidden_grad.astype(F32)
    gate_grad = (
        hidden_grad * up_value * sigmoid_gate * (1.0 + gate_value * (1.0 - sigmoid_gate))
    ).astype(BF16)
    up_grad = (hidden_grad * gate_value * sigmoid_gate).astype(BF16)
    gate_all = lax.all_gather(gate_grad, "row", axis=0, tiled=True)
    up_all = jnp.concatenate(gather_row(up_grad, -1), axis=0)

    hidden_all = jnp.concatenate(hidden_blocks, axis=0)
    down = contract_tokens(turned(cot, row), hidden_all)
    down = halve_core(down.reshape(2, 2, block, hidden_width), core)
    away = swap_far(pick(down, 1 - far, 0).astype(BF16))
    grad_down = pick(down, far, 0) + away.astype(F32)

    gate = contract_tokens(gate_all, tok).reshape(2, 2, -1, features)
    gate = halve_core(gate, core)
    gate_away = pick(gate, 1 - far, 0).astype(BF16)
    up = contract_tokens(up_all, turned(tok, row)).reshape(2, 2, -1, features)
    up = halve_core(up, core)
    up_away = pick(up, 1 - far, 0).astype(BF16)

    from_up = jnp.dot(up_all, w_up, preferred_element_type=F32)
    from_gate = jnp.dot(gate_all, w_gate, preferred_element_type=F32)
    token_grad = (from_gate + turned(from_up, (ROWS - row) & 7)).astype(BF16)
    token_grad = jnp.swapaxes(token_grad.reshape(2, 4, block, features), 0, 1)
    gate_away, up_away, token_grad = lax.optimization_barrier((gate_away, up_away, token_grad))
    grad_gate = pick(gate, far, 0) + swap_far(gate_away).astype(F32)
    grad_up = pick(up, far, 0) + swap_far(up_away).astype(F32)
    over_y = [[a * 4 + b for b in range(4)] for a in range(2)]
    pair = jnp.sum(exchange(token_grad, "col", over_y).astype(F32), axis=0)
    away = swap_x(pick(pair, 1 - x_at, 0).astype(BF16))
    d_tokens = (pick(pair, x_at, 0) + away.astype(F32)).astype(BF16)
    return (d_tokens, grad_gate, grad_up, grad_down)


def solution(mesh):
    placed = (
        P(("dp", "col"), "row"),
        P(("dp", "col"), "row"),
        P(("dp", "row"), "col"),
        P(("dp", "row"), "col"),
        P("col", "row"),
        P("col", "row"),
        P("row", "col"),
    )
    return jax.shard_map(
        local,
        mesh=mesh,
        in_specs=placed,
        out_specs=(
            P(("dp", "col"), "row"),
            P(("col", "dp"), "row"),
            P(("col", "dp"), "row"),
            P(("row", "dp"), "col"),
        ),
        check_vma=False,
    )
```

```python
import jax
import jax.numpy as jnp
from jax import lax
from jax.sharding import PartitionSpec as P

F32 = jnp.float32
BF16 = jnp.bfloat16
ROWS = 8


def shift_row(x, step):
    return lax.ppermute(x, "row", [(i, (i + step) % ROWS) for i in range(ROWS)])


def exchange(x, axis, groups=None):
    return lax.all_to_all(x, axis, 0, 0, axis_index_groups=groups, tiled=True)


def spread_col(x):
    return jnp.broadcast_to(x, (8,) + x.shape)


def pick(x, at, axis):
    return lax.dynamic_index_in_dim(x, at, axis, keepdims=False)


def halve_core(x, core):
    other = lax.ppermute(
        pick(x, 1 - core, 1).astype(BF16), "dp", [(0, 1), (1, 0), (2, 3), (3, 2)]
    )
    return pick(x, core, 1) + other.astype(F32)


def gather_row(x, sign):
    blocks = [None] * ROWS
    blocks[0] = up = down = x
    for step in range(1, 5):
        if step < 4 or sign > 0:
            up = shift_row(up, 1)
            blocks[ROWS - step] = up
        if step < 4 or sign < 0:
            down = shift_row(down, -1)
            blocks[step] = down
    return blocks


def reduce_row(part, later, sooner):
    def add(o, b):
        return (part(o).astype(F32) + b.astype(F32)).astype(BF16)

    up, down = shift_row(part(4), 1), shift_row(part(5), -1)
    up, down, later = lax.optimization_barrier((up, down, later))
    up, down = shift_row(add(3, up), 1), shift_row(add(6, down), -1)
    up, down, sooner = lax.optimization_barrier((up, down, sooner))
    up, down = shift_row(add(2, up), 1), shift_row(add(7, down), -1)
    up = shift_row(add(1, up), 1)
    return part(0).astype(F32) + up.astype(F32) + down.astype(F32), later, sooner


def contract_tokens(left, right):
    return lax.dot_general(left, right, (((0,), (0,)), ((), ())), preferred_element_type=F32)


def local(tokens, cotangent, gate_pre, up_pre, w_gate, w_up, w_down):
    row = lax.axis_index("row")
    dp = lax.axis_index("dp")
    far, core = dp >> 1, dp & 1
    block, hidden_width = gate_pre.shape
    features = w_gate.shape[1]
    width = hidden_width // 2

    def turned(x, by):
        twice = jnp.concatenate([x, x], axis=0)
        return lax.dynamic_slice_in_dim(twice, by * block, ROWS * block, 0)

    def hidden_gradients(hidden_grad, low):
        cols = slice(low, low + width)
        gate_value = gate_pre[:, cols].astype(F32)
        up_value = up_pre[:, cols].astype(F32)
        sigmoid_gate = jax.nn.sigmoid(gate_value)
        gate_grad = hidden_grad * up_value * sigmoid_gate * (1.0 + gate_value * (1.0 - sigmoid_gate))
        up_grad = hidden_grad * gate_value * sigmoid_gate
        return jnp.concatenate([gate_grad.astype(BF16), up_grad.astype(BF16)], axis=1)

    def stacked_weights(low):
        return jnp.concatenate([w_gate[low : low + width], w_up[low : low + width]], axis=0)

    gate_value = gate_pre.astype(F32)
    hidden = (gate_value * jax.nn.sigmoid(gate_value) * up_pre.astype(F32)).astype(BF16)
    hidden_all = lax.all_gather(hidden, "row", axis=0, tiled=True)
    cot = exchange(spread_col(cotangent), "col").reshape(-1, features)

    first = jnp.dot(cot, w_down[:, :width], preferred_element_type=F32).astype(BF16)
    second = jnp.dot(cot, w_down[:, width:], preferred_element_type=F32).astype(BF16)
    parts = first.reshape(ROWS, block, width)
    first_sum, second, hidden_all = reduce_row(
        lambda o: pick(parts, (row + o) & 7, 0), second, hidden_all
    )
    second_sum = lax.psum_scatter(second, "row", scatter_dimension=0, tiled=True)
    first_sum, tokens = lax.optimization_barrier((first_sum, tokens))
    tok = exchange(spread_col(tokens), "col").reshape(-1, features)
    first_blocks = gather_row(hidden_gradients(first_sum, 0), -1)
    second_sum, first_blocks[1], first_blocks[7] = lax.optimization_barrier(
        (second_sum, first_blocks[1], first_blocks[7])
    )
    second_all = lax.all_gather(
        hidden_gradients(second_sum.astype(F32), width), "row", axis=0, tiled=True
    )

    down = contract_tokens(cot, hidden_all)
    down = halve_core(down.reshape(2, 2, block, hidden_width), core)
    away = lax.ppermute(
        pick(down, 1 - far, 0).astype(BF16), "dp", [(0, 2), (2, 0), (1, 3), (3, 1)]
    )
    grad_down = pick(down, far, 0) + away.astype(F32)
    grad_down, first_blocks[4] = lax.optimization_barrier((grad_down, first_blocks[4]))

    first_all = jnp.concatenate(first_blocks, axis=0)
    grads = contract_tokens(first_all, turned(tok, row)).reshape(2, 2, -1, features)
    grads = halve_core(grads, core)
    first_grads = grads + lax.ppermute(grads.astype(BF16), "dp", [(2, 0), (3, 1)]).astype(F32)
    first_token_grad = jnp.dot(first_all, stacked_weights(0), preferred_element_type=F32)
    first_token_grad = turned(first_token_grad, (ROWS - row) & 7)
    second_all, first_grads, first_token_grad = lax.optimization_barrier(
        (second_all, first_grads, first_token_grad)
    )

    grads = lax.optimization_barrier(contract_tokens(second_all, tok))
    grads = halve_core(grads.reshape(2, 2, -1, features), core)
    away = grads.astype(BF16)
    token_grad = jnp.dot(second_all, stacked_weights(width), preferred_element_type=F32)
    token_grad = (token_grad + first_token_grad).astype(BF16)
    second_grads = grads + lax.ppermute(away, "dp", [(0, 2), (1, 3)]).astype(F32)
    token_grad, away = lax.optimization_barrier((token_grad, away))
    token_grad = exchange(token_grad.reshape(8, block, features), "col")
    d_tokens = jnp.sum(token_grad.astype(F32), axis=0).astype(BF16)
    grads = jnp.where(far == 0, first_grads, second_grads)
    return (d_tokens, grads[0], grads[1], grad_down)


def solution(mesh):
    placed = (
        P(("dp", "col"), "row"),
        P(("dp", "col"), "row"),
        P(("dp", "row"), "col"),
        P(("dp", "row"), "col"),
        P("col", "row"),
        P("col", "row"),
        P("row", "col"),
    )
    return jax.shard_map(
        local,
        mesh=mesh,
        in_specs=placed,
        out_specs=(
            P(("dp", "col"), "row"),
            P(("col", "dp"), "row"),
            P(("col", "dp"), "row"),
            P(("row", "dp"), "col"),
        ),
        check_vma=False,
    )
```

```python
import jax
import jax.numpy as jnp
from jax import lax
from jax.sharding import PartitionSpec as P

F32 = jnp.float32
BF16 = jnp.bfloat16
ROWS = 8


def shift_row(x, step):
    return lax.ppermute(x, "row", [(i, (i + step) % ROWS) for i in range(ROWS)])


def swap_far(x):
    return lax.ppermute(x, "dp", [(0, 2), (2, 0), (1, 3), (3, 1)])


def exchange(x, axis, groups=None):
    return lax.all_to_all(x, axis, 0, 0, axis_index_groups=groups, tiled=True)


def spread_col(x):
    return jnp.broadcast_to(x, (8,) + x.shape)


def pick(x, at, axis):
    return lax.dynamic_index_in_dim(x, at, axis, keepdims=False)


def halve_core(x, core):
    other = lax.ppermute(
        pick(x, 1 - core, 1).astype(BF16), "dp", [(0, 1), (1, 0), (2, 3), (3, 2)]
    )
    return pick(x, core, 1) + other.astype(F32)


def gather_row(x, sign):
    blocks = [None] * ROWS
    blocks[0] = up = down = x
    for step in range(1, 5):
        if step < 4 or sign > 0:
            up = shift_row(up, 1)
            blocks[ROWS - step] = up
        if step < 4 or sign < 0:
            down = shift_row(down, -1)
            blocks[step] = down
    return blocks


def reduce_row(part, later, sooner):
    def add(o, b):
        return (part(o).astype(F32) + b.astype(F32)).astype(BF16)

    up, down = shift_row(part(4), 1), shift_row(part(5), -1)
    up, down, later = lax.optimization_barrier((up, down, later))
    up, down = shift_row(add(3, up), 1), shift_row(add(6, down), -1)
    up, down, sooner = lax.optimization_barrier((up, down, sooner))
    up, down = shift_row(add(2, up), 1), shift_row(add(7, down), -1)
    up = shift_row(add(1, up), 1)
    return part(0).astype(F32) + up.astype(F32) + down.astype(F32), later, sooner


def contract_tokens(left, right):
    return lax.dot_general(left, right, (((0,), (0,)), ((), ())), preferred_element_type=F32)


def local(tokens, cotangent, gate_pre, up_pre, w_gate, w_up, w_down):
    row = lax.axis_index("row")
    dp = lax.axis_index("dp")
    far, core = dp >> 1, dp & 1
    block, hidden_width = gate_pre.shape
    features = w_gate.shape[1]

    def turned(x, by):
        twice = jnp.concatenate([x, x], axis=0)
        return lax.dynamic_slice_in_dim(twice, by * block, ROWS * block, 0)

    spread, gate_pre = lax.optimization_barrier((spread_col(cotangent), gate_pre))
    cot = exchange(spread, "col").reshape(-1, features)
    gate_value = gate_pre.astype(F32)
    up_value = up_pre.astype(F32)
    sigmoid_gate = jax.nn.sigmoid(gate_value)
    hidden = (gate_value * sigmoid_gate * up_value).astype(BF16)
    hidden_blocks = gather_row(hidden, 1)
    cot, hidden_blocks[1], hidden_blocks[7] = lax.optimization_barrier(
        (cot, hidden_blocks[1], hidden_blocks[7])
    )
    partial = jnp.dot(cot, w_down, preferred_element_type=F32).astype(BF16)
    parts = partial.reshape(ROWS, block, hidden_width)
    hidden_grad, tokens, hidden_blocks = reduce_row(
        lambda o: pick(parts, (row + o) & 7, 0), tokens, hidden_blocks
    )
    tok = exchange(spread_col(tokens), "col").reshape(-1, features)
    hidden_all = jnp.concatenate(hidden_blocks, axis=0)
    down = contract_tokens(turned(cot, row), hidden_all)
    hidden_grad, tok, down = lax.optimization_barrier((hidden_grad, tok, down))
    up_grad = (hidden_grad * gate_value * sigmoid_gate).astype(BF16)
    gate_grad = (
        hidden_grad * up_value * sigmoid_gate * (1.0 + gate_value * (1.0 - sigmoid_gate))
    ).astype(BF16)
    up_blocks = gather_row(up_grad, -1)
    gate_blocks = gather_row(gate_grad, 1)

    down, up_blocks[1], up_blocks[7] = lax.optimization_barrier((down, up_blocks[1], up_blocks[7]))
    down = halve_core(down.reshape(2, 2, block, hidden_width), core)
    away = swap_far(pick(down, 1 - far, 0).astype(BF16))
    grad_down = pick(down, far, 0) + away.astype(F32)
    grad_down, up_blocks[4] = lax.optimization_barrier((grad_down, up_blocks[4]))

    tok = turned(tok, row)
    up_all = jnp.concatenate(up_blocks, axis=0)
    up = contract_tokens(up_all, tok).reshape(2, 2, -1, features)
    up = halve_core(up, core)
    up_away = swap_far(pick(up, 1 - far, 0).astype(BF16))
    from_up = jnp.dot(up_all, w_up, preferred_element_type=F32)

    gate_all = jnp.concatenate(gate_blocks, axis=0)
    gate = contract_tokens(gate_all, tok).reshape(2, 2, -1, features)
    gate = halve_core(gate, core)
    gate_away = pick(gate, 1 - far, 0).astype(BF16)
    from_gate = jnp.dot(gate_all, w_gate, preferred_element_type=F32)
    token_grad = turned((from_gate + from_up).astype(BF16), (ROWS - row) & 7)
    gate_away, token_grad = lax.optimization_barrier((gate_away, token_grad))
    grad_gate = pick(gate, far, 0) + swap_far(gate_away).astype(F32)
    grad_up = pick(up, far, 0) + up_away.astype(F32)
    token_grad = exchange(token_grad.reshape(8, block, features), "col")
    d_tokens = jnp.sum(token_grad.astype(F32), axis=0).astype(BF16)
    return (d_tokens, grad_gate, grad_up, grad_down)


def solution(mesh):
    placed = (
        P(("dp", "col"), "row"),
        P(("dp", "col"), "row"),
        P(("dp", "row"), "col"),
        P(("dp", "row"), "col"),
        P("col", "row"),
        P("col", "row"),
        P("row", "col"),
    )
    return jax.shard_map(
        local,
        mesh=mesh,
        in_specs=placed,
        out_specs=(
            P(("dp", "col"), "row"),
            P(("col", "dp"), "row"),
            P(("col", "dp"), "row"),
            P(("row", "dp"), "col"),
        ),
        check_vma=False,
    )
```

```python
import jax
import jax.numpy as jnp
from jax import lax
from jax.sharding import PartitionSpec as P

F32 = jnp.float32
BF16 = jnp.bfloat16
ROWS = 8


def shift_row(x, step):
    return lax.ppermute(x, "row", [(i, (i + step) % ROWS) for i in range(ROWS)])


def swap_far(x):
    return lax.ppermute(x, "dp", [(0, 2), (2, 0), (1, 3), (3, 1)])


def swap_x(x):
    return lax.ppermute(x, "col", [(i, (i + 4) % 8) for i in range(8)])


def exchange(x, axis, groups=None):
    return lax.all_to_all(x, axis, 0, 0, axis_index_groups=groups, tiled=True)


def spread_col(x):
    return jnp.broadcast_to(x, (8,) + x.shape)


def pick(x, at, axis):
    return lax.dynamic_index_in_dim(x, at, axis, keepdims=False)


def halve_core(x, core):
    other = lax.ppermute(
        pick(x, 1 - core, 1).astype(BF16), "dp", [(0, 1), (1, 0), (2, 3), (3, 2)]
    )
    return pick(x, core, 1) + other.astype(F32)


def gather_row(x, sign):
    blocks = [None] * ROWS
    blocks[0] = up = down = x
    for step in range(1, 5):
        if step < 4 or sign > 0:
            up = shift_row(up, 1)
            blocks[ROWS - step] = up
        if step < 4 or sign < 0:
            down = shift_row(down, -1)
            blocks[step] = down
    return blocks


def reduce_row(part, later, sooner):
    def add(o, b):
        return (part(o).astype(F32) + b.astype(F32)).astype(BF16)

    up, down = shift_row(part(4), 1), shift_row(part(5), -1)
    up, down, later = lax.optimization_barrier((up, down, later))
    up, down = shift_row(add(3, up), 1), shift_row(add(6, down), -1)
    up, down, sooner = lax.optimization_barrier((up, down, sooner))
    up, down = shift_row(add(2, up), 1), shift_row(add(7, down), -1)
    up = shift_row(add(1, up), 1)
    return part(0).astype(F32) + up.astype(F32) + down.astype(F32), later, sooner


def contract_tokens(left, right):
    return lax.dot_general(left, right, (((0,), (0,)), ((), ())), preferred_element_type=F32)


def local(tokens, cotangent, gate_pre, up_pre, w_gate, w_up, w_down):
    row = lax.axis_index("row")
    dp = lax.axis_index("dp")
    far, core = dp >> 1, dp & 1
    x_at = lax.axis_index("col") >> 2
    block, hidden_width = gate_pre.shape
    features = w_gate.shape[1]

    def placed(blocks):
        whole = jnp.zeros((ROWS * block, hidden_width), BF16)
        for o, x in enumerate(blocks):
            whole = lax.dynamic_update_slice(whole, x, (((row + o) & 7) * block, 0))
        return whole

    spread, gate_pre = lax.optimization_barrier((spread_col(cotangent), gate_pre))
    cot = exchange(spread, "col").reshape(-1, features)
    gate_value = gate_pre.astype(F32)
    up_value = up_pre.astype(F32)
    sigmoid_gate = jax.nn.sigmoid(gate_value)
    hidden = (gate_value * sigmoid_gate * up_value).astype(BF16)
    hidden_blocks = gather_row(hidden, 1)
    cot, hidden_blocks[1], hidden_blocks[7] = lax.optimization_barrier(
        (cot, hidden_blocks[1], hidden_blocks[7])
    )
    partial = jnp.dot(cot, w_down, preferred_element_type=F32).astype(BF16)
    parts = partial.reshape(ROWS, block, hidden_width)
    hidden_grad, tokens, hidden_blocks = reduce_row(
        lambda o: pick(parts, (row + o) & 7, 0), tokens, hidden_blocks
    )
    tok = exchange(spread_col(tokens), "col").reshape(-1, features)
    hidden_all = placed(hidden_blocks)
    down = contract_tokens(cot, hidden_all)
    hidden_grad, tok, down = lax.optimization_barrier((hidden_grad, tok, down))
    up_grad = (hidden_grad * gate_value * sigmoid_gate).astype(BF16)
    up_blocks = gather_row(up_grad, -1)
    hidden_grad, up_blocks[1], up_blocks[7] = lax.optimization_barrier(
        (hidden_grad, up_blocks[1], up_blocks[7])
    )
    gate_grad = (
        hidden_grad * up_value * sigmoid_gate * (1.0 + gate_value * (1.0 - sigmoid_gate))
    ).astype(BF16)
    gate_blocks = gather_row(gate_grad, 1)

    down, up_blocks[2], up_blocks[6] = lax.optimization_barrier((down, up_blocks[2], up_blocks[6]))
    down = halve_core(down.reshape(2, 2, block, hidden_width), core)
    away = swap_far(pick(down, 1 - far, 0).astype(BF16))
    grad_down = pick(down, far, 0) + away.astype(F32)

    up_all = placed(up_blocks)
    up = contract_tokens(up_all, tok).reshape(2, 2, -1, features)
    up = halve_core(up, core)
    up_away = pick(up, 1 - far, 0).astype(BF16)
    from_up = jnp.dot(up_all, w_up, preferred_element_type=F32)
    from_up, up_away, grad_down, gate_blocks[4] = lax.optimization_barrier(
        (from_up, up_away, grad_down, gate_blocks[4])
    )
    up_away = swap_far(up_away)

    gate_all = placed(gate_blocks)
    from_gate = jnp.dot(gate_all, w_gate, preferred_element_type=F32)
    token_grad = (from_gate + from_up).astype(BF16)
    token_grad = jnp.swapaxes(token_grad.reshape(2, 4, block, features), 0, 1)
    gate_all, token_grad = lax.optimization_barrier((gate_all, token_grad))
    over_y = [[a * 4 + b for b in range(4)] for a in range(2)]
    pair = exchange(token_grad, "col", over_y)
    gate = contract_tokens(gate_all, tok).reshape(2, 2, -1, features)
    gate = halve_core(gate, core)
    gate_away = pick(gate, 1 - far, 0).astype(BF16)
    gate_away, up_away = lax.optimization_barrier((gate_away, up_away))
    gate_away = swap_far(gate_away)
    pair = jnp.sum(pair.astype(F32), axis=0)
    away = swap_x(pick(pair, 1 - x_at, 0).astype(BF16))
    d_tokens = (pick(pair, x_at, 0) + away.astype(F32)).astype(BF16)
    grad_up = pick(up, far, 0) + up_away.astype(F32)
    grad_gate = pick(gate, far, 0) + gate_away.astype(F32)
    return (d_tokens, grad_gate, grad_up, grad_down)


def solution(mesh):
    placed = (
        P(("dp", "col"), "row"),
        P(("dp", "col"), "row"),
        P(("dp", "row"), "col"),
        P(("dp", "row"), "col"),
        P("col", "row"),
        P("col", "row"),
        P("row", "col"),
    )
    return jax.shard_map(
        local,
        mesh=mesh,
        in_specs=placed,
        out_specs=(
            P(("dp", "col"), "row"),
            P(("col", "dp"), "row"),
            P(("col", "dp"), "row"),
            P(("row", "dp"), "col"),
        ),
        check_vma=False,
    )
```

```python
import jax
import jax.numpy as jnp
from jax import lax
from jax.experimental import pallas as pl
from jax.experimental.pallas import tpu as pltpu
from jax.sharding import PartitionSpec as P

F32 = jnp.float32
BF16 = jnp.bfloat16
ROWS = 8


def shift_row(x, step):
    return lax.ppermute(x, "row", [(i, (i + step) % ROWS) for i in range(ROWS)])


def swap_far(x):
    return lax.ppermute(x, "dp", [(0, 2), (2, 0), (1, 3), (3, 1)])


def swap_x(x):
    return lax.ppermute(x, "col", [(i, (i + 4) % 8) for i in range(8)])


def exchange(x, axis, groups=None):
    return lax.all_to_all(x, axis, 0, 0, axis_index_groups=groups, tiled=True)


def spread_col(x):
    return jnp.broadcast_to(x, (8,) + x.shape)


def pick(x, at, axis):
    return lax.dynamic_index_in_dim(x, at, axis, keepdims=False)


def halve_core(x, core):
    other = lax.ppermute(
        pick(x, 1 - core, 1).astype(BF16), "dp", [(0, 1), (1, 0), (2, 3), (3, 2)]
    )
    return pick(x, core, 1) + other.astype(F32)


def gather_row(x, sign):
    blocks = [None] * ROWS
    blocks[0] = up = down = x
    for step in range(1, 5):
        if step < 4 or sign > 0:
            up = shift_row(up, 1)
            blocks[ROWS - step] = up
        if step < 4 or sign < 0:
            down = shift_row(down, -1)
            blocks[step] = down
    return blocks


def reduce_row(part, later, sooner):
    def add(o, b):
        return (part(o).astype(F32) + b.astype(F32)).astype(BF16)

    up, down = shift_row(part(4), 1), shift_row(part(5), -1)
    up, down, later = lax.optimization_barrier((up, down, later))
    up, down = shift_row(add(3, up), 1), shift_row(add(6, down), -1)
    up, down, sooner = lax.optimization_barrier((up, down, sooner))
    up, down = shift_row(add(2, up), 1), shift_row(add(7, down), -1)
    up = shift_row(add(1, up), 1)
    return part(0).astype(F32) + up.astype(F32) + down.astype(F32), later, sooner


TILE = 256
TOKENS_FIRST = (((0,), (0,)), ((), ()))


def place_blocks(row_ref, block_refs, whole):
    size = block_refs[0].shape[0]
    for o, ref in enumerate(block_refs):
        at = pl.multiple_of(((row_ref[0] + o) & 7) * size, size)
        whole[pl.ds(at, size), :] = ref[...]
    return whole[...]


def down_kernel(row_ref, *refs):
    *block_refs, cot_ref, out_ref, whole = refs
    hidden = place_blocks(row_ref, block_refs, whole)
    out_ref[...] = lax.dot_general(
        cot_ref[...], hidden, TOKENS_FIRST, preferred_element_type=F32
    )


def up_kernel(row_ref, *refs):
    *block_refs, tok_ref, w_ref, grad_ref, sum_ref, whole = refs
    tile = place_blocks(row_ref, block_refs, whole)
    grad_ref[...] = lax.dot_general(tile, tok_ref[...], TOKENS_FIRST, preferred_element_type=F32)
    part = jnp.dot(tile, w_ref[...], preferred_element_type=F32)

    @pl.when(pl.program_id(0) == 0)
    def _():
        sum_ref[...] = part

    @pl.when(pl.program_id(0) > 0)
    def _():
        sum_ref[...] += part


def gate_kernel(row_ref, *refs):
    *block_refs, tok_ref, w_ref, more_ref, grad_ref, out_ref, whole, total = refs
    tile = place_blocks(row_ref, block_refs, whole)
    grad_ref[...] = lax.dot_general(tile, tok_ref[...], TOKENS_FIRST, preferred_element_type=F32)
    part = jnp.dot(tile, w_ref[...], preferred_element_type=F32)

    @pl.when(pl.program_id(0) == 0)
    def _():
        total[...] = more_ref[...] + part

    @pl.when(pl.program_id(0) > 0)
    def _():
        total[...] += part

    @pl.when(pl.program_id(0) == pl.num_programs(0) - 1)
    def _():
        out_ref[...] = total[...].astype(BF16)


def over_tiles(kernel, row, blocks, wholes, outs, scratch, name):
    block, width = blocks[0].shape
    tokens = ROWS * block
    cols = pl.BlockSpec((block, TILE), lambda j, r: (0, j))

    def whole_spec(shape):
        return pl.BlockSpec(shape, lambda j, r: (0, 0))

    def rows_spec(shape):
        return pl.BlockSpec((TILE, shape[1]), lambda j, r: (j, 0))

    out_specs = []
    for shape, how in outs:
        if how == "rows":
            out_specs.append(rows_spec(shape.shape))
        elif how == "cols":
            out_specs.append(pl.BlockSpec((shape.shape[0], TILE), lambda j, r: (0, j)))
        else:
            out_specs.append(whole_spec(shape.shape))
    before, weights, after = wholes
    in_specs = [cols] * len(blocks) + [whole_spec(x.shape) for x in before]
    in_specs += [rows_spec(x.shape) for x in weights] + [whole_spec(x.shape) for x in after]
    return pl.pallas_call(
        kernel,
        out_shape=[shape for shape, _ in outs],
        grid_spec=pltpu.PrefetchScalarGridSpec(
            num_scalar_prefetch=1,
            grid=(width // TILE,),
            in_specs=in_specs,
            out_specs=out_specs,
            scratch_shapes=[pltpu.VMEM((tokens, TILE), BF16)] + scratch,
        ),
        compiler_params=pltpu.CompilerParams(
            dimension_semantics=("arbitrary",), vmem_limit_bytes=32 << 20
        ),
        name=name,
    )(row, *blocks, *before, *weights, *after)


def local(tokens, cotangent, gate_pre, up_pre, w_gate, w_up, w_down):
    row = lax.axis_index("row")
    dp = lax.axis_index("dp")
    far, core = dp >> 1, dp & 1
    x_at = lax.axis_index("col") >> 2
    block, hidden_width = gate_pre.shape
    features = w_gate.shape[1]

    at_row = row.reshape(1).astype(jnp.int32)
    tokens_by_features = (ROWS * block, features)

    spread, gate_pre = lax.optimization_barrier((spread_col(cotangent), gate_pre))
    cot = exchange(spread, "col").reshape(-1, features)
    gate_value = gate_pre.astype(F32)
    up_value = up_pre.astype(F32)
    sigmoid_gate = jax.nn.sigmoid(gate_value)
    hidden = (gate_value * sigmoid_gate * up_value).astype(BF16)
    hidden_blocks = gather_row(hidden, 1)
    cot, hidden_blocks[1], hidden_blocks[7] = lax.optimization_barrier(
        (cot, hidden_blocks[1], hidden_blocks[7])
    )
    partial = jnp.dot(cot, w_down, preferred_element_type=F32).astype(BF16)
    parts = partial.reshape(ROWS, block, hidden_width)
    hidden_grad, tokens, hidden_blocks = reduce_row(
        lambda o: pick(parts, (row + o) & 7, 0), tokens, hidden_blocks
    )
    tok = exchange(spread_col(tokens), "col").reshape(-1, features)
    (down,) = over_tiles(
        down_kernel,
        at_row,
        hidden_blocks,
        ([cot], [], []),
        [(jax.ShapeDtypeStruct((features, hidden_width), F32), "cols")],
        [],
        "grad_down",
    )
    hidden_grad, tok, down = lax.optimization_barrier((hidden_grad, tok, down))
    up_grad = (hidden_grad * gate_value * sigmoid_gate).astype(BF16)
    gate_grad = (
        hidden_grad * up_value * sigmoid_gate * (1.0 + gate_value * (1.0 - sigmoid_gate))
    ).astype(BF16)
    up_blocks = gather_row(up_grad, -1)
    gate_blocks = gather_row(gate_grad, 1)

    down, up_blocks[1], up_blocks[7] = lax.optimization_barrier((down, up_blocks[1], up_blocks[7]))
    down = halve_core(down.reshape(2, 2, block, hidden_width), core)
    away = swap_far(pick(down, 1 - far, 0).astype(BF16))
    grad_down = pick(down, far, 0) + away.astype(F32)
    grad_down, up_blocks[4] = lax.optimization_barrier((grad_down, up_blocks[4]))

    grad_shape = jax.ShapeDtypeStruct((hidden_width, features), F32)
    up, from_up = over_tiles(
        up_kernel,
        at_row,
        up_blocks,
        ([tok], [w_up], []),
        [(grad_shape, "rows"), (jax.ShapeDtypeStruct(tokens_by_features, F32), "whole")],
        [],
        "grad_up",
    )
    up = halve_core(up.reshape(2, 2, -1, features), core)
    up_away = swap_far(pick(up, 1 - far, 0).astype(BF16))
    gate, token_grad = over_tiles(
        gate_kernel,
        at_row,
        gate_blocks,
        ([tok], [w_gate], [from_up]),
        [(grad_shape, "rows"), (jax.ShapeDtypeStruct(tokens_by_features, BF16), "whole")],
        [pltpu.VMEM(tokens_by_features, F32)],
        "grad_gate",
    )
    gate = halve_core(gate.reshape(2, 2, -1, features), core)
    gate_away = pick(gate, 1 - far, 0).astype(BF16)
    token_grad = jnp.swapaxes(token_grad.reshape(2, 4, block, features), 0, 1)
    over_y = [[a * 4 + b for b in range(4)] for a in range(2)]
    pair = exchange(token_grad, "col", over_y)
    gate_sent = swap_far(gate_away)
    pair, gate_away, up_away = lax.optimization_barrier((pair, gate_away, up_away))
    grad_up = pick(up, far, 0) + up_away.astype(F32)
    pair = jnp.sum(pair.astype(F32), axis=0)
    away = swap_x(pick(pair, 1 - x_at, 0).astype(BF16))
    d_tokens = (pick(pair, x_at, 0) + away.astype(F32)).astype(BF16)
    grad_gate = pick(gate, far, 0) + gate_sent.astype(F32)
    return (d_tokens, grad_gate, grad_up, grad_down)


def solution(mesh):
    placed = (
        P(("dp", "col"), "row"),
        P(("dp", "col"), "row"),
        P(("dp", "row"), "col"),
        P(("dp", "row"), "col"),
        P("col", "row"),
        P("col", "row"),
        P("row", "col"),
    )
    return jax.shard_map(
        local,
        mesh=mesh,
        in_specs=placed,
        out_specs=(
            P(("dp", "col"), "row"),
            P(("col", "dp"), "row"),
            P(("col", "dp"), "row"),
            P(("row", "dp"), "col"),
        ),
        check_vma=False,
    )
```

```python
import jax
import jax.numpy as jnp
from jax import lax
from jax.sharding import PartitionSpec as P

F32 = jnp.float32
BF16 = jnp.bfloat16
ROWS = 8


def shift_row(x, step):
    return lax.ppermute(x, "row", [(i, (i + step) % ROWS) for i in range(ROWS)])


def swap_far(x):
    return lax.ppermute(x, "dp", [(0, 2), (2, 0), (1, 3), (3, 1)])


def swap_x(x):
    return lax.ppermute(x, "col", [(i, (i + 4) % 8) for i in range(8)])


def exchange(x, axis, groups=None):
    return lax.all_to_all(x, axis, 0, 0, axis_index_groups=groups, tiled=True)


def spread_col(x):
    return jnp.broadcast_to(x, (8,) + x.shape)


def pick(x, at, axis):
    return lax.dynamic_index_in_dim(x, at, axis, keepdims=False)


def halve_core(x, core):
    other = lax.ppermute(
        pick(x, 1 - core, 1).astype(BF16), "dp", [(0, 1), (1, 0), (2, 3), (3, 2)]
    )
    return pick(x, core, 1) + other.astype(F32)


def gather_row(x, sign):
    blocks = [None] * ROWS
    blocks[0] = up = down = x
    for step in range(1, 5):
        if step < 4 or sign > 0:
            up = shift_row(up, 1)
            blocks[ROWS - step] = up
        if step < 4 or sign < 0:
            down = shift_row(down, -1)
            blocks[step] = down
    return blocks


def reduce_row(part, later, sooner, sign):
    def add(o, b):
        return (part(o).astype(F32) + b.astype(F32)).astype(BF16)

    if sign > 0:
        up, down = shift_row(part(4), 1), shift_row(part(5), -1)
        up, down, later = lax.optimization_barrier((up, down, later))
        up, down = shift_row(add(3, up), 1), shift_row(add(6, down), -1)
        up, down, sooner = lax.optimization_barrier((up, down, sooner))
        up, down = shift_row(add(2, up), 1), shift_row(add(7, down), -1)
        up = shift_row(add(1, up), 1)
    else:
        up, down = shift_row(part(3), 1), shift_row(part(4), -1)
        up, down, later = lax.optimization_barrier((up, down, later))
        up, down = shift_row(add(2, up), 1), shift_row(add(5, down), -1)
        up, down, sooner = lax.optimization_barrier((up, down, sooner))
        up, down = shift_row(add(1, up), 1), shift_row(add(6, down), -1)
        down = shift_row(add(7, down), -1)
    return part(0).astype(F32) + up.astype(F32) + down.astype(F32), later, sooner


def contract_tokens(left, right):
    return lax.dot_general(left, right, (((0,), (0,)), ((), ())), preferred_element_type=F32)


def local(tokens, cotangent, gate_pre, up_pre, w_gate, w_up, w_down):
    row = lax.axis_index("row")
    dp = lax.axis_index("dp")
    far, core = dp >> 1, dp & 1
    x_at = lax.axis_index("col") >> 2
    block, hidden_width = gate_pre.shape
    features = w_gate.shape[1]

    def turned(x, by):
        twice = jnp.concatenate([x, x], axis=0)
        return lax.dynamic_slice_in_dim(twice, by * block, ROWS * block, 0)

    spread, gate_pre = lax.optimization_barrier((spread_col(cotangent), gate_pre))
    cot = exchange(spread, "col").reshape(-1, features)
    gate_value = gate_pre.astype(F32)
    up_value = up_pre.astype(F32)
    sigmoid_gate = jax.nn.sigmoid(gate_value)
    hidden = (gate_value * sigmoid_gate * up_value).astype(BF16)
    hidden_blocks = gather_row(hidden, 1)
    cot, hidden_blocks[1], hidden_blocks[7] = lax.optimization_barrier(
        (cot, hidden_blocks[1], hidden_blocks[7])
    )
    partial = jnp.dot(cot, w_down, preferred_element_type=F32).astype(BF16)
    parts = partial.reshape(ROWS, block, hidden_width)
    half = hidden_width // 2
    left, tokens, hidden_blocks = reduce_row(
        lambda o: pick(parts, (row + o) & 7, 0)[:, :half], tokens, hidden_blocks, 1
    )
    right, _, hidden_blocks = reduce_row(
        lambda o: pick(parts, (row + o) & 7, 0)[:, half:], [], hidden_blocks, -1
    )
    hidden_grad = jnp.concatenate([left, right], axis=1)
    tok = exchange(spread_col(tokens), "col").reshape(-1, features)
    hidden_all = jnp.concatenate(hidden_blocks, axis=0)
    down = contract_tokens(turned(cot, row), hidden_all)
    hidden_grad, tok, down = lax.optimization_barrier((hidden_grad, tok, down))
    up_grad = (hidden_grad * gate_value * sigmoid_gate).astype(BF16)
    gate_grad = (
        hidden_grad * up_value * sigmoid_gate * (1.0 + gate_value * (1.0 - sigmoid_gate))
    ).astype(BF16)
    up_blocks = gather_row(up_grad, -1)
    gate_blocks = gather_row(gate_grad, 1)

    down, up_blocks[1], up_blocks[7] = lax.optimization_barrier((down, up_blocks[1], up_blocks[7]))
    down = halve_core(down.reshape(2, 2, block, hidden_width), core)
    away = swap_far(pick(down, 1 - far, 0).astype(BF16))
    grad_down = pick(down, far, 0) + away.astype(F32)
    grad_down, up_blocks[4] = lax.optimization_barrier((grad_down, up_blocks[4]))

    tok = turned(tok, row)
    up_all = jnp.concatenate(up_blocks, axis=0)
    up = contract_tokens(up_all, tok).reshape(2, 2, -1, features)
    up = halve_core(up, core)
    up_away = pick(up, 1 - far, 0).astype(BF16)
    from_up = jnp.dot(up_all, w_up, preferred_element_type=F32)

    gate_all = jnp.concatenate(gate_blocks, axis=0)
    gate = contract_tokens(gate_all, tok).reshape(2, 2, -1, features)
    gate_all, up_away = lax.optimization_barrier((gate_all, up_away))
    up_sent = swap_far(up_away)
    gate = halve_core(gate, core)
    gate_away = pick(gate, 1 - far, 0).astype(BF16)
    gate_sent = swap_far(gate_away)
    from_gate = jnp.dot(gate_all, w_gate, preferred_element_type=F32)
    token_grad = turned((from_gate + from_up).astype(BF16), (ROWS - row) & 7)
    token_grad = jnp.swapaxes(token_grad.reshape(2, 4, block, features), 0, 1)
    token_grad, up_sent = lax.optimization_barrier((token_grad, up_sent))
    over_y = [[a * 4 + b for b in range(4)] for a in range(2)]
    pair = exchange(token_grad, "col", over_y)
    pair, gate_away = lax.optimization_barrier((pair, gate_away))
    pair = jnp.sum(pair.astype(F32), axis=0)
    away = swap_x(pick(pair, 1 - x_at, 0).astype(BF16))
    d_tokens = (pick(pair, x_at, 0) + away.astype(F32)).astype(BF16)
    grad_up = pick(up, far, 0) + up_sent.astype(F32)
    grad_gate = pick(gate, far, 0) + gate_sent.astype(F32)
    return (d_tokens, grad_gate, grad_up, grad_down)


def solution(mesh):
    placed = (
        P(("dp", "col"), "row"),
        P(("dp", "col"), "row"),
        P(("dp", "row"), "col"),
        P(("dp", "row"), "col"),
        P("col", "row"),
        P("col", "row"),
        P("row", "col"),
    )
    return jax.shard_map(
        local,
        mesh=mesh,
        in_specs=placed,
        out_specs=(
            P(("dp", "col"), "row"),
            P(("col", "dp"), "row"),
            P(("col", "dp"), "row"),
            P(("row", "dp"), "col"),
        ),
        check_vma=False,
    )
```

```python
import jax
import jax.numpy as jnp
from jax import lax
from jax.sharding import PartitionSpec as P

F32 = jnp.float32
BF16 = jnp.bfloat16
ROWS = 8


def shift_row(x, step):
    return lax.ppermute(x, "row", [(i, (i + step) % ROWS) for i in range(ROWS)])


def swap_far(x):
    return lax.ppermute(x, "dp", [(0, 2), (2, 0), (1, 3), (3, 1)])


def swap_x(x):
    return lax.ppermute(x, "col", [(i, (i + 4) % 8) for i in range(8)])


def exchange(x, axis, groups=None):
    return lax.all_to_all(x, axis, 0, 0, axis_index_groups=groups, tiled=True)


def spread_col(x):
    return jnp.broadcast_to(x, (8,) + x.shape)


def pick(x, at, axis):
    return lax.dynamic_index_in_dim(x, at, axis, keepdims=False)


def halve_core(x, core):
    other = lax.ppermute(
        pick(x, 1 - core, 1).astype(BF16), "dp", [(0, 1), (1, 0), (2, 3), (3, 2)]
    )
    return pick(x, core, 1) + other.astype(F32)


def gather_row(x, sign):
    blocks = [None] * ROWS
    blocks[0] = up = down = x
    for step in range(1, 5):
        if step < 4 or sign > 0:
            up = shift_row(up, 1)
            blocks[ROWS - step] = up
        if step < 4 or sign < 0:
            down = shift_row(down, -1)
            blocks[step] = down
    return blocks


def reduce_row(part, later, sooner):
    def add(o, b):
        return (part(o).astype(F32) + b.astype(F32)).astype(BF16)

    up, down = shift_row(part(4), 1), shift_row(part(5), -1)
    up, down, later = lax.optimization_barrier((up, down, later))
    up, down = shift_row(add(3, up), 1), shift_row(add(6, down), -1)
    up, down, sooner = lax.optimization_barrier((up, down, sooner))
    up, down = shift_row(add(2, up), 1), shift_row(add(7, down), -1)
    up = shift_row(add(1, up), 1)
    return part(0).astype(F32) + up.astype(F32) + down.astype(F32), later, sooner


def contract_tokens(left, right):
    return lax.dot_general(left, right, (((0,), (0,)), ((), ())), preferred_element_type=F32)


def local(tokens, cotangent, gate_pre, up_pre, w_gate, w_up, w_down):
    row = lax.axis_index("row")
    dp = lax.axis_index("dp")
    far, core = dp >> 1, dp & 1
    x_at = lax.axis_index("col") >> 2
    block, hidden_width = gate_pre.shape
    features = w_gate.shape[1]

    def turned(x, by):
        twice = jnp.concatenate([x, x], axis=0)
        return lax.dynamic_slice_in_dim(twice, by * block, ROWS * block, 0)

    spread, gate_pre = lax.optimization_barrier((spread_col(cotangent), gate_pre))
    cot = exchange(spread, "col").reshape(-1, features)
    gate_value = gate_pre.astype(F32)
    up_value = up_pre.astype(F32)
    sigmoid_gate = jax.nn.sigmoid(gate_value)
    hidden = (gate_value * sigmoid_gate * up_value).astype(BF16)
    hidden_blocks = gather_row(hidden, 1)
    cot, hidden_blocks[1], hidden_blocks[7] = lax.optimization_barrier(
        (cot, hidden_blocks[1], hidden_blocks[7])
    )
    partial = jnp.dot(cot, w_down, preferred_element_type=F32).astype(BF16)
    parts = partial.reshape(ROWS, block, hidden_width)
    sooner = hidden_blocks[:4] + hidden_blocks[5:]
    hidden_grad, tokens, sooner = reduce_row(
        lambda o: pick(parts, (row + o) & 7, 0), tokens, sooner
    )
    hidden_blocks = sooner[:4] + hidden_blocks[4:5] + sooner[4:]
    tok = exchange(spread_col(tokens), "col").reshape(-1, features)
    hidden_all = jnp.concatenate(hidden_blocks, axis=0)
    down = contract_tokens(turned(cot, row), hidden_all)
    hidden_grad, tok, down = lax.optimization_barrier((hidden_grad, tok, down))
    up_grad = (hidden_grad * gate_value * sigmoid_gate).astype(BF16)
    gate_grad = (
        hidden_grad * up_value * sigmoid_gate * (1.0 + gate_value * (1.0 - sigmoid_gate))
    ).astype(BF16)
    up_blocks = gather_row(up_grad, -1)
    gate_blocks = gather_row(gate_grad, 1)

    down, up_blocks[1], up_blocks[7] = lax.optimization_barrier((down, up_blocks[1], up_blocks[7]))
    down = halve_core(down.reshape(2, 2, block, hidden_width), core)
    away = swap_far(pick(down, 1 - far, 0).astype(BF16))
    grad_down = pick(down, far, 0) + away.astype(F32)
    grad_down, up_blocks[4] = lax.optimization_barrier((grad_down, up_blocks[4]))

    tok = turned(tok, row)
    up_all = jnp.concatenate(up_blocks, axis=0)
    up = contract_tokens(up_all, tok).reshape(2, 2, -1, features)
    up = halve_core(up, core)
    up_away = pick(up, 1 - far, 0).astype(BF16)
    from_up = jnp.dot(up_all, w_up, preferred_element_type=F32)

    gate_all = jnp.concatenate(gate_blocks, axis=0)
    gate = contract_tokens(gate_all, tok).reshape(2, 2, -1, features)
    gate = halve_core(gate, core)
    gate_away = pick(gate, 1 - far, 0).astype(BF16)
    gate_all, up_away, gate_away = lax.optimization_barrier((gate_all, up_away, gate_away))
    up_sent, gate_sent = swap_far(up_away), swap_far(gate_away)
    from_gate = jnp.dot(gate_all, w_gate, preferred_element_type=F32)
    token_grad = turned((from_gate + from_up).astype(BF16), (ROWS - row) & 7)
    token_grad = jnp.swapaxes(token_grad.reshape(2, 4, block, features), 0, 1)
    token_grad, up_sent = lax.optimization_barrier((token_grad, up_sent))
    over_y = [[a * 4 + b for b in range(4)] for a in range(2)]
    pair = exchange(token_grad, "col", over_y)
    pair, gate_away = lax.optimization_barrier((pair, gate_away))
    pair = jnp.sum(pair.astype(F32), axis=0)
    away = swap_x(pick(pair, 1 - x_at, 0).astype(BF16))
    d_tokens = (pick(pair, x_at, 0) + away.astype(F32)).astype(BF16)
    grad_up = pick(up, far, 0) + up_sent.astype(F32)
    grad_gate = pick(gate, far, 0) + gate_sent.astype(F32)
    return (d_tokens, grad_gate, grad_up, grad_down)


def solution(mesh):
    placed = (
        P(("dp", "col"), "row"),
        P(("dp", "col"), "row"),
        P(("dp", "row"), "col"),
        P(("dp", "row"), "col"),
        P("col", "row"),
        P("col", "row"),
        P("row", "col"),
    )
    return jax.shard_map(
        local,
        mesh=mesh,
        in_specs=placed,
        out_specs=(
            P(("dp", "col"), "row"),
            P(("col", "dp"), "row"),
            P(("col", "dp"), "row"),
            P(("row", "dp"), "col"),
        ),
        check_vma=False,
    )
```

```python
import jax
import jax.numpy as jnp
from jax import lax
from jax.sharding import PartitionSpec as P

F32 = jnp.float32
BF16 = jnp.bfloat16
ROWS = 8


def shift_row(x, step):
    return lax.ppermute(x, "row", [(i, (i + step) % ROWS) for i in range(ROWS)])


def swap_far(x):
    return lax.ppermute(x, "dp", [(0, 2), (2, 0), (1, 3), (3, 1)])


def exchange(x, axis, groups=None):
    return lax.all_to_all(x, axis, 0, 0, axis_index_groups=groups, tiled=True)


def spread_col(x):
    return jnp.broadcast_to(x, (8,) + x.shape)


def pick(x, at, axis):
    return lax.dynamic_index_in_dim(x, at, axis, keepdims=False)


def halve_core(x, core, axis):
    other = lax.ppermute(
        pick(x, 1 - core, axis).astype(BF16), "dp", [(0, 1), (1, 0), (2, 3), (3, 2)]
    )
    return pick(x, core, axis) + other.astype(F32)


def gather_row(x, sign):
    blocks = [None] * ROWS
    blocks[0] = up = down = x
    for step in range(1, 4):
        up, down = shift_row(up, 1), shift_row(down, -1)
        blocks[ROWS - step], blocks[step] = up, down
    half = x.shape[0] // 2
    if sign > 0:
        blocks[4] = shift_row(up, 1)
    else:
        blocks[4:5] = [shift_row(up[:half], 1), shift_row(down[half:], -1)]
    return blocks


def reduce_row(part, later, sooner):
    def add(o, b):
        return (part(o).astype(F32) + b.astype(F32)).astype(BF16)

    up, down = shift_row(part(4), 1), shift_row(part(5), -1)
    up, down, later = lax.optimization_barrier((up, down, later))
    up, down = shift_row(add(3, up), 1), shift_row(add(6, down), -1)
    up, down, sooner = lax.optimization_barrier((up, down, sooner))
    up, down = shift_row(add(2, up), 1), shift_row(add(7, down), -1)
    up = shift_row(add(1, up), 1)
    return part(0).astype(F32) + up.astype(F32) + down.astype(F32), later, sooner


def contract_tokens(left, right):
    return lax.dot_general(left, right, (((0,), (0,)), ((), ())), preferred_element_type=F32)


def local(tokens, cotangent, gate_pre, up_pre, w_gate, w_up, w_down):
    row = lax.axis_index("row")
    dp = lax.axis_index("dp")
    far, core = dp >> 1, dp & 1
    block, hidden_width = gate_pre.shape
    features = w_gate.shape[1]

    def turned(x, by):
        twice = jnp.concatenate([x, x], axis=0)
        return lax.dynamic_slice_in_dim(twice, by * block, ROWS * block, 0)

    spread, gate_pre = lax.optimization_barrier((spread_col(cotangent), gate_pre))
    cot = exchange(spread, "col").reshape(-1, features)
    gate_value = gate_pre.astype(F32)
    up_value = up_pre.astype(F32)
    sigmoid_gate = jax.nn.sigmoid(gate_value)
    hidden = (gate_value * sigmoid_gate * up_value).astype(BF16)
    hidden_blocks = gather_row(hidden, 1)
    weights = jnp.concatenate([w_up, w_gate], axis=0)
    cot, weights, hidden_blocks[1], hidden_blocks[7] = lax.optimization_barrier(
        (cot, weights, hidden_blocks[1], hidden_blocks[7])
    )
    partial = jnp.dot(cot, w_down, preferred_element_type=F32).astype(BF16)
    parts = partial.reshape(ROWS, block, hidden_width)
    hidden_grad, tokens, hidden_blocks = reduce_row(
        lambda o: pick(parts, (row + o) & 7, 0), tokens, hidden_blocks
    )
    tok = exchange(spread_col(tokens), "col").reshape(-1, features)
    hidden_all = jnp.concatenate(hidden_blocks, axis=0)
    down = contract_tokens(turned(cot, row), hidden_all)
    hidden_grad, tok, down = lax.optimization_barrier((hidden_grad, tok, down))
    up_grad = (hidden_grad * gate_value * sigmoid_gate).astype(BF16)
    gate_grad = (
        hidden_grad * up_value * sigmoid_gate * (1.0 + gate_value * (1.0 - sigmoid_gate))
    ).astype(BF16)
    blocks = gather_row(jnp.concatenate([up_grad, gate_grad], axis=1), 0)

    down = halve_core(down.reshape(2, 2, block, hidden_width), core, 1)
    away = swap_far(pick(down, 1 - far, 0).astype(BF16))
    grad_down = pick(down, far, 0) + away.astype(F32)
    grad_down, blocks[4] = lax.optimization_barrier((grad_down, blocks[4]))

    both = jnp.concatenate(blocks, axis=0)
    grads = contract_tokens(both, turned(tok, row)).reshape(2, 2, 2, -1, features)
    grads = halve_core(grads, core, 2)
    away = pick(grads, 1 - far, 1).astype(BF16)
    token_grad = jnp.dot(both, weights, preferred_element_type=F32).astype(BF16)
    token_grad = turned(token_grad, (ROWS - row) & 7)
    token_grad = token_grad.reshape(8, block, features)
    away, token_grad = lax.optimization_barrier((away, token_grad))
    grads = pick(grads, far, 1) + swap_far(away).astype(F32)
    token_grad = exchange(token_grad, "col")
    d_tokens = jnp.sum(token_grad.astype(F32), axis=0).astype(BF16)
    return (d_tokens, grads[1], grads[0], grad_down)


def solution(mesh):
    placed = (
        P(("dp", "col"), "row"),
        P(("dp", "col"), "row"),
        P(("dp", "row"), "col"),
        P(("dp", "row"), "col"),
        P("col", "row"),
        P("col", "row"),
        P("row", "col"),
    )
    return jax.shard_map(
        local,
        mesh=mesh,
        in_specs=placed,
        out_specs=(
            P(("dp", "col"), "row"),
            P(("col", "dp"), "row"),
            P(("col", "dp"), "row"),
            P(("row", "dp"), "col"),
        ),
        check_vma=False,
    )
```

```python
import jax
import jax.numpy as jnp
from jax import lax
from jax.sharding import PartitionSpec as P

F32 = jnp.float32
BF16 = jnp.bfloat16
ROWS = 8


def shift_row(x, step):
    return lax.ppermute(x, "row", [(i, (i + step) % ROWS) for i in range(ROWS)])


def swap_far(x):
    return lax.ppermute(x, "dp", [(0, 2), (2, 0), (1, 3), (3, 1)])


def swap_x(x):
    return lax.ppermute(x, "col", [(i, (i + 4) % 8) for i in range(8)])


def exchange(x, axis, groups=None):
    return lax.all_to_all(x, axis, 0, 0, axis_index_groups=groups, tiled=True)


def spread_col(x):
    return jnp.broadcast_to(x, (8,) + x.shape)


def pick(x, at, axis):
    return lax.dynamic_index_in_dim(x, at, axis, keepdims=False)


def halve_core(x, core):
    other = lax.ppermute(
        pick(x, 1 - core, 1).astype(BF16), "dp", [(0, 1), (1, 0), (2, 3), (3, 2)]
    )
    return pick(x, core, 1) + other.astype(F32)


def gather_row(x, sign):
    blocks = [None] * ROWS
    blocks[0] = up = down = x
    for step in range(1, 5):
        if step < 4 or sign > 0:
            up = shift_row(up, 1)
            blocks[ROWS - step] = up
        if step < 4 or sign < 0:
            down = shift_row(down, -1)
            blocks[step] = down
    return blocks


def reduce_row(part, later, sooner):
    def add(o, b):
        return (part(o).astype(F32) + b.astype(F32)).astype(BF16)

    up, down = shift_row(part(4), 1), shift_row(part(5), -1)
    up, down, later = lax.optimization_barrier((up, down, later))
    up, down = shift_row(add(3, up), 1), shift_row(add(6, down), -1)
    up, down, sooner = lax.optimization_barrier((up, down, sooner))
    up, down = shift_row(add(2, up), 1), shift_row(add(7, down), -1)
    up = shift_row(add(1, up), 1)
    return part(0).astype(F32) + up.astype(F32) + down.astype(F32), later, sooner


def contract_tokens(left, right):
    return lax.dot_general(left, right, (((0,), (0,)), ((), ())), preferred_element_type=F32)


def local(tokens, cotangent, gate_pre, up_pre, w_gate, w_up, w_down):
    row = lax.axis_index("row")
    dp = lax.axis_index("dp")
    far, core = dp >> 1, dp & 1
    x_at = lax.axis_index("col") >> 2
    block, hidden_width = gate_pre.shape
    features = w_gate.shape[1]

    def turned(x, by):
        twice = jnp.concatenate([x, x], axis=0)
        return lax.dynamic_slice_in_dim(twice, by * block, ROWS * block, 0)

    spread, gate_pre = lax.optimization_barrier((spread_col(cotangent), gate_pre))
    cot = exchange(spread, "col").reshape(-1, features)
    gate_value = gate_pre.astype(F32)
    up_value = up_pre.astype(F32)
    sigmoid_gate = jax.nn.sigmoid(gate_value)
    hidden = (gate_value * sigmoid_gate * up_value).astype(BF16)
    hidden_blocks = gather_row(hidden, 1)
    cot, hidden_blocks[1], hidden_blocks[7] = lax.optimization_barrier(
        (cot, hidden_blocks[1], hidden_blocks[7])
    )
    partial = jnp.dot(cot, w_down, preferred_element_type=F32).astype(BF16)
    parts = partial.reshape(ROWS, block, hidden_width)
    hidden_grad, tokens, hidden_blocks = reduce_row(
        lambda o: pick(parts, (row + o) & 7, 0), tokens, hidden_blocks
    )
    tok = exchange(spread_col(tokens), "col").reshape(-1, features)
    hidden_all = jnp.concatenate(hidden_blocks, axis=0)
    down = contract_tokens(turned(cot, row), hidden_all)
    hidden_grad, tok, down = lax.optimization_barrier((hidden_grad, tok, down))
    up_grad = (hidden_grad * gate_value * sigmoid_gate).astype(BF16)
    gate_grad = (
        hidden_grad * up_value * sigmoid_gate * (1.0 + gate_value * (1.0 - sigmoid_gate))
    ).astype(BF16)
    up_blocks = gather_row(up_grad, -1)
    gate_blocks = gather_row(gate_grad, 1)

    down, up_blocks[1], up_blocks[7] = lax.optimization_barrier((down, up_blocks[1], up_blocks[7]))
    down = halve_core(down.reshape(2, 2, block, hidden_width), core)
    away = swap_far(pick(down, 1 - far, 0).astype(BF16))
    grad_down = pick(down, far, 0) + away.astype(F32)
    grad_down, up_blocks[4] = lax.optimization_barrier((grad_down, up_blocks[4]))

    tok = turned(tok, row)
    up_all = jnp.concatenate(up_blocks, axis=0)
    up = contract_tokens(up_all, tok).reshape(2, 2, -1, features)
    up = halve_core(up, core)
    up_away = swap_far(pick(up, 1 - far, 0).astype(BF16))
    from_up = jnp.dot(up_all, w_up, preferred_element_type=F32)

    gate_all = jnp.concatenate(gate_blocks, axis=0)
    gate = contract_tokens(gate_all, tok).reshape(2, 2, -1, features)
    gate = halve_core(gate, core)
    gate_away = pick(gate, 1 - far, 0).astype(BF16)
    from_gate = jnp.dot(gate_all, w_gate, preferred_element_type=F32)
    token_grad = turned((from_gate + from_up).astype(BF16), (ROWS - row) & 7)
    token_grad = jnp.swapaxes(token_grad.reshape(2, 4, block, features), 0, 1)
    gate_away, token_grad = lax.optimization_barrier((gate_away, token_grad))
    grad_gate = pick(gate, far, 0) + swap_far(gate_away).astype(F32)
    grad_up = pick(up, far, 0) + up_away.astype(F32)
    over_y = [[a * 4 + b for b in range(4)] for a in range(2)]
    pair = jnp.sum(exchange(token_grad, "col", over_y).astype(F32), axis=0)
    away = swap_x(pick(pair, 1 - x_at, 0).astype(BF16))
    d_tokens = (pick(pair, x_at, 0) + away.astype(F32)).astype(BF16)
    return (d_tokens, grad_gate, grad_up, grad_down)


def solution(mesh):
    placed = (
        P(("dp", "col"), "row"),
        P(("dp", "col"), "row"),
        P(("dp", "row"), "col"),
        P(("dp", "row"), "col"),
        P("col", "row"),
        P("col", "row"),
        P("row", "col"),
    )
    return jax.shard_map(
        local,
        mesh=mesh,
        in_specs=placed,
        out_specs=(
            P(("dp", "col"), "row"),
            P(("col", "dp"), "row"),
            P(("col", "dp"), "row"),
            P(("row", "dp"), "col"),
        ),
        check_vma=False,
    )
```

```python
import jax
import jax.numpy as jnp
from jax import lax
from jax.sharding import PartitionSpec as P

F32 = jnp.float32
BF16 = jnp.bfloat16
ROWS = 8


def shift_row(x, step):
    return lax.ppermute(x, "row", [(i, (i + step) % ROWS) for i in range(ROWS)])


def swap_far(x):
    return lax.ppermute(x, "dp", [(0, 2), (2, 0), (1, 3), (3, 1)])


def swap_x(x):
    return lax.ppermute(x, "col", [(i, (i + 4) % 8) for i in range(8)])


def exchange(x, axis, groups=None):
    return lax.all_to_all(x, axis, 0, 0, axis_index_groups=groups, tiled=True)


def spread_col(x):
    return jnp.broadcast_to(x, (8,) + x.shape)


def pick(x, at, axis):
    return lax.dynamic_index_in_dim(x, at, axis, keepdims=False)


def halve_core(x, core):
    other = lax.ppermute(
        pick(x, 1 - core, 1).astype(BF16), "dp", [(0, 1), (1, 0), (2, 3), (3, 2)]
    )
    return pick(x, core, 1) + other.astype(F32)


def gather_row(x, sign):
    blocks = [None] * ROWS
    blocks[0] = up = down = x
    for step in range(1, 5):
        if step < 4 or sign > 0:
            up = shift_row(up, 1)
            blocks[ROWS - step] = up
        if step < 4 or sign < 0:
            down = shift_row(down, -1)
            blocks[step] = down
    return blocks


def reduce_row(part, later, sooner):
    def add(o, b):
        return (part(o).astype(F32) + b.astype(F32)).astype(BF16)

    up, down = shift_row(part(4), 1), shift_row(part(5), -1)
    up, down, later = lax.optimization_barrier((up, down, later))
    up, down = shift_row(add(3, up), 1), shift_row(add(6, down), -1)
    up, down, sooner = lax.optimization_barrier((up, down, sooner))
    up, down = shift_row(add(2, up), 1), shift_row(add(7, down), -1)
    up = shift_row(add(1, up), 1)
    return part(0).astype(F32) + up.astype(F32) + down.astype(F32), later, sooner


def contract_tokens(left, right):
    return lax.dot_general(left, right, (((0,), (0,)), ((), ())), preferred_element_type=F32)


def local(tokens, cotangent, gate_pre, up_pre, w_gate, w_up, w_down):
    row = lax.axis_index("row")
    dp = lax.axis_index("dp")
    far, core = dp >> 1, dp & 1
    x_at = lax.axis_index("col") >> 2
    block, hidden_width = gate_pre.shape
    features = w_gate.shape[1]

    def turned(x, by):
        twice = jnp.concatenate([x, x], axis=0)
        return lax.dynamic_slice_in_dim(twice, by * block, ROWS * block, 0)

    spread, gate_pre = lax.optimization_barrier((spread_col(cotangent), gate_pre))
    cot = exchange(spread, "col").reshape(-1, features)
    gate_value = gate_pre.astype(F32)
    up_value = up_pre.astype(F32)
    sigmoid_gate = jax.nn.sigmoid(gate_value)
    hidden = (gate_value * sigmoid_gate * up_value).astype(BF16)
    hidden_blocks = gather_row(hidden, 1)
    cot, hidden_blocks[1], hidden_blocks[7] = lax.optimization_barrier(
        (cot, hidden_blocks[1], hidden_blocks[7])
    )
    partial = jnp.dot(cot, w_down, preferred_element_type=F32).astype(BF16)
    parts = partial.reshape(ROWS, block, hidden_width)
    hidden_grad, tokens, hidden_blocks = reduce_row(
        lambda o: pick(parts, (row + o) & 7, 0), tokens, hidden_blocks
    )
    tok = exchange(spread_col(tokens), "col").reshape(-1, features)
    hidden_all = jnp.concatenate(hidden_blocks, axis=0)
    down = contract_tokens(turned(cot, row), hidden_all)
    hidden_grad, tok, down = lax.optimization_barrier((hidden_grad, tok, down))
    up_grad = (hidden_grad * gate_value * sigmoid_gate).astype(BF16)
    gate_grad = (
        hidden_grad * up_value * sigmoid_gate * (1.0 + gate_value * (1.0 - sigmoid_gate))
    ).astype(BF16)
    up_blocks = gather_row(up_grad, -1)
    gate_blocks = gather_row(gate_grad, 1)

    down, up_blocks[1], up_blocks[7] = lax.optimization_barrier((down, up_blocks[1], up_blocks[7]))
    down = halve_core(down.reshape(2, 2, block, hidden_width), core)
    away = swap_far(pick(down, 1 - far, 0).astype(BF16))
    grad_down = pick(down, far, 0) + away.astype(F32)
    grad_down, up_blocks[4] = lax.optimization_barrier((grad_down, up_blocks[4]))

    tok = turned(tok, row)
    up_all = jnp.concatenate(up_blocks, axis=0)
    up = contract_tokens(up_all, tok).reshape(2, 2, -1, features)
    up = halve_core(up, core)
    up_away = pick(up, 1 - far, 0).astype(BF16)
    from_up = jnp.dot(up_all, w_up, preferred_element_type=F32)

    gate_all = jnp.concatenate(gate_blocks, axis=0)
    gate = contract_tokens(gate_all, tok).reshape(2, 2, -1, features)
    gate = halve_core(gate, core)
    gate_away = pick(gate, 1 - far, 0).astype(BF16)
    from_gate = jnp.dot(gate_all, w_gate, preferred_element_type=F32)
    token_grad = turned((from_gate + from_up).astype(BF16), (ROWS - row) & 7)
    token_grad = jnp.swapaxes(token_grad.reshape(2, 4, block, features), 0, 1)
    gate_away, up_away, token_grad = lax.optimization_barrier((gate_away, up_away, token_grad))
    up_away = swap_far(up_away)
    grad_gate = pick(gate, far, 0) + swap_far(gate_away).astype(F32)
    grad_up = pick(up, far, 0) + up_away.astype(F32)
    over_y = [[a * 4 + b for b in range(4)] for a in range(2)]
    pair = jnp.sum(exchange(token_grad, "col", over_y).astype(F32), axis=0)
    away = swap_x(pick(pair, 1 - x_at, 0).astype(BF16))
    d_tokens = (pick(pair, x_at, 0) + away.astype(F32)).astype(BF16)
    return (d_tokens, grad_gate, grad_up, grad_down)


def solution(mesh):
    placed = (
        P(("dp", "col"), "row"),
        P(("dp", "col"), "row"),
        P(("dp", "row"), "col"),
        P(("dp", "row"), "col"),
        P("col", "row"),
        P("col", "row"),
        P("row", "col"),
    )
    return jax.shard_map(
        local,
        mesh=mesh,
        in_specs=placed,
        out_specs=(
            P(("dp", "col"), "row"),
            P(("col", "dp"), "row"),
            P(("col", "dp"), "row"),
            P(("row", "dp"), "col"),
        ),
        check_vma=False,
    )
```
